32 devices in a mesh: verts: 8 (over z, y), modes: 4 (over x, core).
Axes of the slice: x: 2, y: 2, z: 4, core: 2. Of those that a mesh axis runs over, the one named last changes fastest.
Arguments:
- reduced_coords: float32 [256], P('modes'), may hold values from -4 to 4
- mode_basis: bfloat16 [256, 3, 8192], P('modes', None, 'verts'), may hold values from -0.375 to 0.375
- rest_shape: float32 [3, 8192], P(None, 'verts'), may hold values from -6 to 6
- stiffness: float32 [8192], P('verts'), may hold values from 0.2 to 2
- send_slots: int32 [8, 8, 16], P('verts'), may hold values from 0 to 1023
- pair_peer: int32 [8, 2, 1024], P('verts'), may hold values from 0 to 7
- pair_slot: int32 [8, 2, 1024], P('verts'), may hold values from 0 to 15
- pair_count: int32 [8], P('verts'), may hold values from 1 to 1024, 4096 in all
Outputs:
- hessian: float32 [256, 256], P('modes')
- gradient: float32 [256], P('modes')
The draws below stay inside these ranges and needn't reach their ends.
Inputs may be any that keep to these rules, and one draw needn't show every extreme that they name: `send_slots`: indices may repeat. `pair_count`: the counts sum to 8 * 512 and the busiest owner has all 1024 slots live; slots at and beyond an owner's count hold valid but unused indices.
All inputs are finite; a program needn't handle non-finite values. No bound on the sum of `pair_count` on one device may be relied on, other than what follows from the above.
Results may differ from the reference program's by a relative error of at most 0.0046.
Values may be sent and summed in bfloat16 or wider, within the bound.
No kernel may reach another device: no remote copies, remote signals or barrier semaphores. Data moves between devices by JAX's collectives and lax.ppermute only.
A program may use at most 64 MiB of HBM per device.

```python
import math
import jax
import jax.numpy as jnp
import numpy as np
from jax import lax

M = 256
VB = 1024
C = 16
P_SIZE = 1024
V = 8192
N_VERTS = 8


def plant(result, stream_key, least, high):
    longest = result.shape.index(max(result.shape))
    spots = []
    for shift in (0, 1):
        where = [jax.random.randint(jax.random.fold_in(stream_key, axis), (), 0, length) for axis, length in enumerate(result.shape)]
        where[longest] = (where[longest] + shift) % result.shape[longest]
        spots.append(tuple(where))
    return result.at[spots[0]].set(least).at[spots[1]].set(high)


def levels(key, dims, split, smallest, high):
    def one(position, shards_of):
        heights = jax.random.uniform(jax.random.fold_in(jax.random.fold_in(key, 6), position), (shards_of,), jnp.float32, smallest / len(split), high / len(split))
        return jnp.repeat(jnp.exp(heights), dims[position] // shards_of).reshape((-1,) + (1,) * (len(dims) - position - 1))

    gain = one(*split[0])
    for cut in split[1:]:
        gain = gain * one(*cut)
    return gain


def profile(count, total, bound, slope):
    weights = [(1 << 20) // math.isqrt(rank ** slope) + 1 for rank in range(2, count + 1)]
    surplus, holding = total - bound - (count - 1), [1] * (count - 1)
    while surplus > 0:
        free = [i for i in range(count - 1) if holding[i] < bound]
        mass, left = sum([weights[i] for i in free]), surplus
        for i in free:
            addition = min(bound - holding[i], max(1, left * weights[i] // mass), surplus)
            holding[i] = holding[i] + addition
            surplus = surplus - addition
    return np.array([bound] + holding)


def uneven_parts(key, count, total, bound, slope):
    if count == 2:
        one = jax.random.randint(key, (), max(1, total - bound), min(bound, total - 1) + 1)
        return jnp.stack([one, total - one])
    tallies = jnp.asarray(profile(count, total, bound, slope), jnp.int32)
    twos = (count - 1) // 2
    source_of, taker = tallies[1:1 + 2 * twos:2], tallies[2:2 + 2 * twos:2]
    room = jnp.minimum(source_of - 1, bound - taker)
    moved = jax.random.randint(jax.random.fold_in(key, 1), (twos,), 0, 1 << 20) % (room + 1)
    tallies = tallies.at[1:1 + 2 * twos:2].set(source_of - moved).at[2:2 + 2 * twos:2].set(taker + moved)
    return tallies[jax.random.permutation(jax.random.fold_in(key, 2), count)]


def normal_values(own_key, dims, deviation, reach, cuts=(), held_as=jnp.bfloat16):
    result = deviation * jax.random.normal(own_key, dims, jnp.float32)
    if cuts:
        result = result * levels(own_key, dims, cuts, -0.22, 0.18)
    return jnp.clip(result, -reach, reach).astype(held_as)


def setup_inputs(seed: int = 0) -> dict:
    streams_of = jax.random.split(jax.random.key(seed), 9)
    reduced_coords = normal_values(streams_of[0], (M,), 0.3, 4.0, ((0, 4),), jnp.float32)
    mode_basis = normal_values(streams_of[1], (M, 3, V), M ** -0.5, 0.375, ((0, 4), (2, 8)))
    rest_shape = normal_values(streams_of[2], (3, V), 0.5, 6.0, ((1, 8),), jnp.float32)
    stiffness = jnp.clip(jnp.exp(math.log(2.0) - 2.3025851 * jax.random.uniform(streams_of[3], (V,), jnp.float32) ** levels(streams_of[3], (V,), ((0, 8),), -0.2, 0.2)), 0.2, 2.0)
    send_slots = plant(jax.random.randint(streams_of[4], (N_VERTS, N_VERTS, C), 0, VB), jax.random.fold_in(streams_of[4], 1), 0, VB - 1).astype(jnp.int32)
    pair_peer = plant(jax.random.randint(streams_of[5], (N_VERTS, 2, P_SIZE), 0, N_VERTS), jax.random.fold_in(streams_of[5], 1), 0, N_VERTS - 1).astype(jnp.int32)
    pair_slot = plant(jax.random.randint(streams_of[6], (N_VERTS, 2, P_SIZE), 0, C), jax.random.fold_in(streams_of[6], 1), 0, C - 1).astype(jnp.int32)
    pair_count = uneven_parts(streams_of[7], N_VERTS, N_VERTS * P_SIZE // 2, P_SIZE, 2).astype(jnp.int32)
    return {"reduced_coords": reduced_coords, "mode_basis": mode_basis, "rest_shape": rest_shape, "stiffness": stiffness, "send_slots": send_slots, "pair_peer": pair_peer, "pair_slot": pair_slot, "pair_count": pair_count}


highest = lax.Precision.HIGHEST
barrier_reach = 1.5
gap_offset = 0.1

def barrier_slopes(distance):
    excess = distance - barrier_reach
    ratio_log = jnp.log(distance / barrier_reach)
    slope_term = -(2.0 * excess * ratio_log + excess * excess / distance)
    curvature = -(2.0 * ratio_log + 4.0 * excess / distance - excess * excess / (distance * distance))
    inside = distance < barrier_reach
    return (jnp.where(inside, slope_term, 0.0), jnp.where(inside, curvature, 0.0))

def outer_sum(left_rows, right_rows):
    return lax.dot_general(left_rows.astype(jnp.float32), right_rows.astype(jnp.float32), (((1,), (1,)), ((), ())), precision=highest, preferred_element_type=jnp.float32)

def spring_terms(displacement, stiffness):
    radius = jnp.sqrt(1.0 + lax.optimization_barrier(jnp.sum(displacement * displacement, axis=0)))
    spring_rate = stiffness / radius
    return (spring_rate, -spring_rate / (radius * radius), spring_rate * displacement)

def elastic_left(basis_block, displacement, spring_rate, curvature_rate):
    mode_count, _, vertex_count = basis_block.shape
    projected = lax.optimization_barrier(jnp.sum(basis_block.astype(jnp.float32) * displacement[None], axis=1))
    scaled = (spring_rate * basis_block.astype(jnp.float32)).astype(jnp.bfloat16)
    return jnp.concatenate([scaled.reshape(mode_count, 3 * vertex_count), (curvature_rate * projected).astype(jnp.bfloat16)], axis=1)

def elastic_right(basis_block, displacement):
    mode_count, _, vertex_count = basis_block.shape
    projected = lax.optimization_barrier(jnp.sum(basis_block.astype(jnp.float32) * displacement[None], axis=1))
    return jnp.concatenate([basis_block.reshape(mode_count, 3 * vertex_count), projected.astype(jnp.bfloat16)], axis=1)

def contact_terms(rows_first, rows_second, separation, active):
    mode_count, _, slot_total = rows_first.shape
    distance = lax.optimization_barrier(jnp.sum(separation * separation, axis=0)) + gap_offset
    slope_term, curvature = barrier_slopes(distance)
    slope_term = slope_term * active
    curvature = curvature * active
    difference = rows_first.astype(jnp.float32) - rows_second.astype(jnp.float32)
    leverage = lax.optimization_barrier(jnp.sum(difference * separation[None], axis=1))
    left_rows = jnp.concatenate([(2.0 * slope_term * difference).astype(jnp.bfloat16).reshape(mode_count, 3 * slot_total), (4.0 * curvature * leverage).astype(jnp.bfloat16)], axis=1)
    right_rows = jnp.concatenate([difference.astype(jnp.bfloat16).reshape(mode_count, 3 * slot_total), leverage.astype(jnp.bfloat16)], axis=1)
    contact_grad = lax.optimization_barrier(jnp.sum(difference * (2.0 * slope_term * separation)[None], axis=(1, 2)))
    return (left_rows, right_rows, contact_grad)

def reference(reduced_coords, mode_basis, rest_shape, stiffness, send_slots, pair_peer, pair_slot, pair_count):
    mode_count = mode_basis.shape[0]
    total = rest_shape.shape[1]
    blocks = N_VERTS
    vertex_count = total // blocks
    slot_total = pair_peer.shape[2]

    def rebuild(block_index):
        first_row = block_index * vertex_count
        basis_block = lax.dynamic_slice_in_dim(mode_basis, first_row, vertex_count, 2)
        rest_block = lax.dynamic_slice_in_dim(rest_shape, first_row, vertex_count, 1)
        moved = jnp.dot(reduced_coords, basis_block.reshape(mode_count, 3 * vertex_count).astype(jnp.float32), precision=highest, preferred_element_type=jnp.float32)
        return rest_block + moved.reshape(3, vertex_count)
    stacked = lax.map(rebuild, jnp.arange(blocks, dtype=jnp.int32))
    positions = jnp.transpose(stacked, (1, 0, 2)).reshape(3, total)

    def elastic_step(totals, block_index):
        first_row = block_index * vertex_count
        basis_block = lax.dynamic_slice_in_dim(mode_basis, first_row, vertex_count, 2)
        rest_block = lax.dynamic_slice_in_dim(rest_shape, first_row, vertex_count, 1)
        stiff_block = lax.dynamic_slice_in_dim(stiffness, first_row, vertex_count, 0)
        displacement = stacked[block_index] - rest_block
        spring_rate, curvature_rate, elastic_force = spring_terms(displacement, stiff_block)
        left_rows = elastic_left(basis_block, displacement, spring_rate, curvature_rate)
        right_rows = elastic_right(basis_block, displacement)
        grad_term = jnp.dot(basis_block.reshape(mode_count, 3 * vertex_count).astype(jnp.float32), elastic_force.reshape(3 * vertex_count), precision=highest, preferred_element_type=jnp.float32)
        return ((totals[0] + outer_sum(left_rows, right_rows), totals[1] + grad_term), None)
    initial = (jnp.zeros((mode_count, mode_count), jnp.float32), jnp.zeros((mode_count,), jnp.float32))
    totals, _ = lax.scan(elastic_step, initial, jnp.arange(blocks, dtype=jnp.int32))

    def contact_step(totals, owner_index):
        senders = pair_peer[owner_index]
        chosen = send_slots[senders, owner_index, pair_slot[owner_index]]
        vertex_ids = (senders * vertex_count + chosen).reshape(-1).astype(jnp.int32)
        pos_ends = jnp.take(positions, vertex_ids, axis=1).reshape(3, 2, slot_total)
        row_ends = jnp.take(mode_basis, vertex_ids, axis=2).reshape(mode_count, 3, 2, slot_total)
        separation = pos_ends[:, 0] - pos_ends[:, 1]
        active = (jnp.arange(slot_total, dtype=jnp.int32) < pair_count[owner_index]).astype(jnp.float32)
        left_rows, right_rows, contact_grad = contact_terms(row_ends[:, :, 0], row_ends[:, :, 1], separation, active)
        return ((totals[0] + outer_sum(left_rows, right_rows), totals[1] + contact_grad), None)
    totals, _ = lax.scan(contact_step, totals, jnp.arange(blocks, dtype=jnp.int32))
    factor = mode_count / (3.0 * total)
    return (totals[0] * factor, totals[1] * factor)
```

```python
import jax
import jax.numpy as jnp
from jax import lax
from jax.experimental import pallas as pl
from jax.experimental.pallas import tpu as pltpu
from jax.sharding import PartitionSpec as P


barrier_reach = 1.5
gap_offset = 0.1
f32, bf16 = jnp.float32, jnp.bfloat16

NT = (((1,), (1,)), ((), ()))
NN = (((1,), (0,)), ((), ()))
TN = (((0,), (0,)), ((), ()))
VM = pl.BlockSpec(memory_space=pltpu.VMEM)
SM = pl.BlockSpec(memory_space=pltpu.SMEM)


def mm(a, b, dims):
    return lax.dot_general(a, b, dims, preferred_element_type=f32)


def parts_of(x):
    high = x.astype(bf16)
    rest = x - high.astype(f32)
    middle = rest.astype(bf16)
    low = (rest - middle.astype(f32)).astype(bf16)
    return [high, middle, low]


def stack_rows(rows, count):
    width = rows[0].shape[1]
    have = len(rows)
    return jnp.concatenate(rows + [jnp.zeros((count - have, width), rows[0].dtype)], axis=0)


def barrier_slopes(distance):
    excess = distance - barrier_reach
    ratio_log = jnp.log(distance / barrier_reach)
    slope_term = -(2.0 * excess * ratio_log + excess * excess / distance)
    curvature = -(
        2.0 * ratio_log + 4.0 * excess / distance - excess * excess / (distance * distance)
    )
    inside = distance < barrier_reach
    return (jnp.where(inside, slope_term, 0.0), jnp.where(inside, curvature, 0.0))


def swap_blocks(h, step, width):
    size = step * width
    pieces = [h[:, i : i + size] for i in range(0, h.shape[1], size)]
    order = [pieces[i ^ 1] for i in range(len(pieces))]
    return jnp.concatenate(order, axis=1)


def permute_static(h, p, groups, width):
    step = 1
    while step < groups:
        if p & step:
            h = swap_blocks(h, step, width)
        step *= 2
    return h


def permute_traced(h, m, groups, width):
    step = 1
    while step < groups:
        h = jnp.where((m & step) != 0, swap_blocks(h, step, width), h)
        step *= 2
    return h


def select_kernel(groups, q_ref, basis_ref, rest_ref, slots_ref, *refs):
    outs, con_ref, rows_ref = refs[:groups], refs[groups], refs[groups + 1]
    comps, local, count = basis_ref.shape
    quarter = count // groups
    m = lax.axis_index("modes")
    q_rows = stack_rows(parts_of(q_ref[...]), 16)
    q_rows = jnp.concatenate([q_rows, jnp.zeros((16, quarter - local), bf16)], axis=1)
    for p in range(groups):
        base = pl.multiple_of((m ^ p) * quarter, quarter)
        for k in range(comps):
            outs[p][k * local : (k + 1) * local, :] = basis_ref[k, :, pl.ds(base, quarter)]
        outs[p][comps * local :, :] = q_rows
    for k in range(comps):
        rows_ref[k * local : (k + 1) * local, :] = basis_ref[k]
    rest_rows = []
    for k in range(comps):
        rest_rows += parts_of(rest_ref[k : k + 1, :])
    rows_ref[comps * local :, :] = stack_rows(rest_rows, rows_ref.shape[0] - comps * local)
    slots = slots_ref[...]
    peers, slot_count = slots.shape
    spread = jnp.broadcast_to(slots[:, None, :], (peers, slot_count, slot_count))
    pick = lax.broadcasted_iota(jnp.int32, spread.shape, 1) == lax.broadcasted_iota(
        jnp.int32, spread.shape, 2
    )
    column = jnp.sum(jnp.where(pick, spread, 0).astype(f32), axis=2, keepdims=True)
    column = column.reshape(peers * slot_count, 1).astype(jnp.int32)
    hot = lax.broadcasted_iota(jnp.int32, (peers * slot_count, count), 1) == column
    hot = jnp.where(hot, 1.0, 0.0).astype(bf16)
    con_ref[...] = mm(hot, rows_ref[...], NT).astype(bf16)


def elastic_kernel(groups, nodes, *refs):
    msgs = refs[:groups]
    stiff_ref, con_ref = refs[groups], refs[groups + 1]
    own_ref, qs_ref = refs[groups + 2], refs[groups + 3]
    outs = refs[groups + 4 : groups + 3 + groups]
    right_ref, left_ref = refs[groups + 3 + groups :]
    quarter = msgs[0].shape[1]
    local = own_ref.shape[0] - 8
    comps = 3
    m = lax.axis_index("modes")
    disp = []
    for k in range(comps):
        total = None
        for p in range(groups):
            q_rows = msgs[p][comps * local : comps * local + 16, :local]
            term = mm(q_rows, msgs[p][k * local : (k + 1) * local, :], NN)
            total = term if total is None else total + term
        disp.append(total[0:1] + total[1:2] + total[2:3])
    for p in range(groups):
        qs_ref[:, p * local : (p + 1) * local] = msgs[p][comps * local : comps * local + 16, :local]
    square = 1.0 + (disp[0] * disp[0] + disp[1] * disp[1] + disp[2] * disp[2])
    radius = jnp.sqrt(square)
    base = pl.multiple_of(m * quarter, quarter)
    spring_rate = stiff_ref[:, pl.ds(base, quarter)] / radius
    curvature_rate = -spring_rate / (radius * radius)
    for p in range(groups):
        rows = slice(p * local, (p + 1) * local)
        projected = None
        for k in range(comps):
            block = msgs[p][k * local : (k + 1) * local, :]
            wide = block.astype(f32)
            right_ref[rows, k * quarter : (k + 1) * quarter] = block
            left_ref[rows, k * quarter : (k + 1) * quarter] = (spring_rate * wide).astype(bf16)
            term = wide * disp[k]
            projected = term if projected is None else projected + term
        right_ref[rows, comps * quarter :] = projected.astype(bf16)
        left_ref[rows, comps * quarter :] = (curvature_rate * projected).astype(bf16)
    hess = mm(left_ref[...], right_ref[...], NT)
    force = [spring_rate * d for d in disp]
    force_rows = jnp.concatenate([stack_rows(parts_of(f), 16) for f in force], axis=1)
    grads = mm(force_rows, right_ref[:, : comps * quarter], NT)
    grad = grads[0:1] + grads[1:2] + grads[2:3]
    width = groups * local
    own_ref[:local, :] = hess[:local]
    own_ref[local:, :] = stack_rows([permute_static(grad, 0, groups, local)], 8)
    for p in range(1, groups):
        out = outs[p - 1]
        out[:nodes, :] = con_ref[...]
        out[nodes : nodes + local, :] = permute_static(
            hess[p * local : (p + 1) * local], p, groups, local
        ).astype(bf16)
        out[nodes + local :, :] = stack_rows(
            parts_of(permute_static(grad, p, groups, local)), 16
        )


def contact_kernel(groups, slot_count, factor, *refs):
    con_ref = refs[0]
    msgs = refs[1:groups]
    own_ref, qs_ref, peer_ref, slot_ref, count_ref = refs[groups : groups + 5]
    out_ref, right_ref, left_ref = refs[groups + 5 :]
    nodes = con_ref.shape[0]
    local = own_ref.shape[0] - 8
    comps = 3
    pairs = peer_ref.shape[1]
    m = lax.axis_index("modes")
    blocks = [con_ref] + list(msgs)
    position = lax.broadcasted_iota(jnp.int32, (1, pairs), 1)
    live = position < count_ref[0]
    ends = peer_ref[...] * slot_count + slot_ref[...]
    node = lax.broadcasted_iota(jnp.int32, (nodes, pairs), 0)
    first = jnp.where((node == ends[0:1]) & live, 1.0, 0.0)
    second = jnp.where((node == ends[1:2]) & live, 1.0, 0.0)
    edge = (first - second).astype(bf16)
    lane = lax.broadcasted_iota(jnp.int32, (16, local), 1)
    row = lax.broadcasted_iota(jnp.int32, (16, local), 0)
    pick = jnp.where((lane >= 3 * row) & (lane < 3 * row + 3), 1.0, 0.0).astype(bf16)
    rest = mm(pick, con_ref[:, comps * local :], NT)
    rows = []
    for k in range(comps):
        total = None
        for p in range(groups):
            term = mm(
                qs_ref[:, p * local : (p + 1) * local],
                blocks[p][:nodes, k * local : (k + 1) * local],
                NT,
            )
            total = term if total is None else total + term
        moved = total[0:1] + total[1:2] + total[2:3]
        rows += parts_of(rest[k : k + 1] + moved)
    gaps = mm(stack_rows(rows, 16), edge, NN)
    sep = [gaps[3 * k : 3 * k + 1] + gaps[3 * k + 1 : 3 * k + 2] + gaps[3 * k + 2 : 3 * k + 3] for k in range(comps)]
    distance = sep[0] * sep[0] + sep[1] * sep[1] + sep[2] * sep[2] + gap_offset
    slope, bend = barrier_slopes(distance)
    active = jnp.where(live, 1.0, 0.0)
    slope = slope * active
    bend = bend * active
    for p in range(groups):
        diff = mm(blocks[p][:nodes, : comps * local], edge, TN)
        rows_p = slice(p * local, (p + 1) * local)
        leverage = None
        for k in range(comps):
            part = diff[k * local : (k + 1) * local]
            right_ref[rows_p, k * pairs : (k + 1) * pairs] = part.astype(bf16)
            if p == 0:
                left_ref[:, k * pairs : (k + 1) * pairs] = (2.0 * slope * part).astype(bf16)
            term = part * sep[k]
            leverage = term if leverage is None else leverage + term
        right_ref[rows_p, comps * pairs :] = leverage.astype(bf16)
        if p == 0:
            left_ref[:, comps * pairs :] = (4.0 * bend * leverage).astype(bf16)
    hess = own_ref[:local, :] + mm(left_ref[...], right_ref[...], NT)
    force_rows = []
    for k in range(comps):
        force_rows += parts_of(2.0 * slope * sep[k])
    spread = mm(stack_rows(force_rows, 16), edge, NT)
    node_rows = []
    for k in range(comps):
        node_rows += parts_of(spread[3 * k : 3 * k + 1] + spread[3 * k + 1 : 3 * k + 2] + spread[3 * k + 2 : 3 * k + 3])
    pulled = mm(stack_rows(node_rows, 16), con_ref[:, : comps * local], NN)
    grad = own_ref[local : local + 1, :local]
    for k in range(comps):
        for i in range(3):
            grad = grad + pulled[3 * k + i : 3 * k + i + 1, k * local : (k + 1) * local]
    for p in range(1, groups):
        got = msgs[p - 1]
        hess = hess + got[nodes : nodes + local, :].astype(f32)
        for i in range(3):
            grad = grad + got[nodes + local : nodes + local + 16, :local].astype(f32)[i : i + 1]
    hess = permute_traced(hess, m, groups, local)
    out_ref[:local, :] = (hess * factor).astype(bf16)
    grad_rows = stack_rows(parts_of(grad * factor), 16)
    out_ref[local:, :] = jnp.concatenate(
        [grad_rows, jnp.zeros((16, out_ref.shape[1] - local), bf16)], axis=1
    )


def body(
    reduced_coords, mode_basis, rest_shape, stiffness, send_slots, pair_peer, pair_slot, pair_count
):
    local, comps, count = mode_basis.shape
    peers = lax.axis_size("verts")
    groups = lax.axis_size("modes")
    modes = local * groups
    factor = modes / (3.0 * count * peers)
    quarter = count // groups
    slot_count = send_slots.shape[2]
    nodes = peers * slot_count
    pairs = pair_peer.shape[2]
    msg_rows = comps * local + 16
    wide = (comps + 1) * local

    def swap(x, axis, step):
        size = lax.axis_size(axis)
        return lax.ppermute(x, axis, [(i, i ^ step) for i in range(size)])

    def limit(n):
        return pltpu.CompilerParams(vmem_limit_bytes=n)

    *mine, contact = pl.pallas_call(
        lambda *refs: select_kernel(groups, *refs),
        out_shape=[jax.ShapeDtypeStruct((msg_rows, quarter), bf16)] * groups
        + [jax.ShapeDtypeStruct((nodes, wide), bf16)],
        in_specs=[VM] * 4,
        out_specs=[VM] * (groups + 1),
        scratch_shapes=[pltpu.VMEM((wide, count), bf16)],
        compiler_params=limit((8 if nodes <= 256 else 40) << 20),
        name="select",
    )(
        reduced_coords.reshape(1, local),
        jnp.transpose(mode_basis, (1, 0, 2)),
        rest_shape,
        send_slots[0],
    )
    contact = lax.all_to_all(
        contact.reshape(peers, slot_count, wide), "verts", split_axis=0, concat_axis=0, tiled=True
    ).reshape(nodes, wide)
    basis = [mine[0]] + [swap(mine[p], "modes", p) for p in range(1, groups)]
    own, coords, *sends = pl.pallas_call(
        lambda *refs: elastic_kernel(groups, nodes, *refs),
        out_shape=[
            jax.ShapeDtypeStruct((local + 8, modes), f32),
            jax.ShapeDtypeStruct((16, modes), bf16),
        ]
        + [jax.ShapeDtypeStruct((nodes + local + 16, modes), bf16)] * (groups - 1),
        in_specs=[VM] * (groups + 2),
        out_specs=[VM] * (groups + 1),
        scratch_shapes=[pltpu.VMEM((modes, (comps + 1) * quarter), bf16)] * 2,
        compiler_params=limit((8 if nodes <= 256 else 40) << 20),
        name="elastic",
    )(*basis, stiffness.reshape(1, count), contact)
    got = [swap(sends[p - 1], "modes", p) for p in range(1, groups)]
    total = pl.pallas_call(
        lambda *refs: contact_kernel(groups, slot_count, factor, *refs),
        out_shape=jax.ShapeDtypeStruct((local + 16, modes), bf16),
        in_specs=[VM] * (groups + 4) + [SM],
        out_specs=VM,
        scratch_shapes=[
            pltpu.VMEM((modes, (comps + 1) * pairs), bf16),
            pltpu.VMEM((local, (comps + 1) * pairs), bf16),
        ],
        compiler_params=limit((16 if nodes <= 256 else 56) << 20),
        name="contact",
    )(contact, *got, own, coords, pair_peer[0], pair_slot[0], pair_count)

    step = 1
    while step < peers:
        other = swap(total, "verts", step)
        hess = total[:local].astype(f32) + other[:local].astype(f32)
        rows = total[local : local + 3, :local].astype(f32) + other[local : local + 3, :local].astype(f32)
        grad = rows[0] + (rows[1] + rows[2])
        step *= 2
        if step < peers:
            high = lax.reduce_precision(grad, 8, 7)
            middle = lax.reduce_precision(grad - high, 8, 7)
            low = grad - high - middle
            grads = jnp.pad(jnp.stack([high, middle, low]), ((0, 13), (0, modes - local)))
            total = jnp.concatenate([hess, grads], axis=0).astype(bf16)
    return (hess, grad)


def solution(mesh):
    return jax.shard_map(
        body,
        mesh=mesh,
        in_specs=(
            P("modes"),
            P("modes", None, "verts"),
            P(None, "verts"),
            P("verts"),
            P("verts", None, None),
            P("verts", None, None),
            P("verts", None, None),
            P("verts"),
        ),
        out_specs=(P("modes", None), P("modes")),
        check_vma=False,
    )
```

```python
import jax
import jax.numpy as jnp
from jax import lax
from jax.experimental import pallas as pl
from jax.experimental.pallas import tpu as pltpu
from jax.sharding import PartitionSpec as P


barrier_reach = 1.5
gap_offset = 0.1
f32, bf16 = jnp.float32, jnp.bfloat16

NT = (((1,), (1,)), ((), ()))
NN = (((1,), (0,)), ((), ()))
TN = (((0,), (0,)), ((), ()))
VM = pl.BlockSpec(memory_space=pltpu.VMEM)
SM = pl.BlockSpec(memory_space=pltpu.SMEM)
HB = pl.BlockSpec(memory_space=pltpu.HBM)


def mm(a, b, dims):
    return lax.dot_general(a, b, dims, preferred_element_type=f32)


def parts_of(x):
    high = x.astype(bf16)
    rest = x - high.astype(f32)
    middle = rest.astype(bf16)
    low = (rest - middle.astype(f32)).astype(bf16)
    return [high, middle, low]


def stack_rows(rows, count):
    width = rows[0].shape[1]
    have = len(rows)
    return jnp.concatenate(rows + [jnp.zeros((count - have, width), rows[0].dtype)], axis=0)


def barrier_slopes(distance):
    excess = distance - barrier_reach
    ratio_log = jnp.log(distance / barrier_reach)
    slope_term = -(2.0 * excess * ratio_log + excess * excess / distance)
    curvature = -(
        2.0 * ratio_log + 4.0 * excess / distance - excess * excess / (distance * distance)
    )
    inside = distance < barrier_reach
    return (jnp.where(inside, slope_term, 0.0), jnp.where(inside, curvature, 0.0))


def swap_blocks(h, step, width):
    size = step * width
    pieces = [h[:, i : i + size] for i in range(0, h.shape[1], size)]
    order = [pieces[i ^ 1] for i in range(len(pieces))]
    return jnp.concatenate(order, axis=1)


def permute_static(h, p, groups, width):
    step = 1
    while step < groups:
        if p & step:
            h = swap_blocks(h, step, width)
        step *= 2
    return h


def permute_traced(h, m, groups, width):
    step = 1
    while step < groups:
        h = jnp.where((m & step) != 0, swap_blocks(h, step, width), h)
        step *= 2
    return h


def select_kernel(groups, q_hbm, basis_hbm, rest_hbm, slots_hbm, *refs):
    outs, con_ref = refs[:groups], refs[groups]
    rows_ref, q_ref, basis_ref, rest_ref, slots_ref, sems = refs[groups + 1 :]
    comps, local, count = basis_ref.shape
    quarter = count // groups
    copies = [
        pltpu.make_async_copy(slots_hbm, slots_ref, sems.at[0]),
        pltpu.make_async_copy(rest_hbm, rest_ref, sems.at[1]),
        pltpu.make_async_copy(q_hbm, q_ref, sems.at[2]),
        pltpu.make_async_copy(basis_hbm, basis_ref, sems.at[3]),
    ]
    for copy in copies:
        copy.start()
    copies[0].wait()
    slots = slots_ref[...]
    peers, slot_count = slots.shape
    spread = jnp.broadcast_to(slots[:, None, :], (peers, slot_count, slot_count))
    pick = lax.broadcasted_iota(jnp.int32, spread.shape, 1) == lax.broadcasted_iota(
        jnp.int32, spread.shape, 2
    )
    column = jnp.sum(jnp.where(pick, spread, 0).astype(f32), axis=2, keepdims=True)
    column = column.reshape(peers * slot_count, 1).astype(jnp.int32)
    hot = lax.broadcasted_iota(jnp.int32, (peers * slot_count, count), 1) == column
    hot = jnp.where(hot, 1.0, 0.0).astype(bf16)
    copies[1].wait()
    rest_rows = []
    for k in range(comps):
        rest_rows += parts_of(rest_ref[k : k + 1, :])
    rows_ref[comps * local :, :] = stack_rows(rest_rows, rows_ref.shape[0] - comps * local)
    copies[2].wait()
    m = lax.axis_index("modes")
    q_rows = stack_rows(parts_of(q_ref[...]), 16)
    q_rows = jnp.concatenate([q_rows, jnp.zeros((16, quarter - local), bf16)], axis=1)
    for p in range(groups):
        outs[p][comps * local :, :] = q_rows
    copies[3].wait()
    for k in range(comps):
        rows_ref[k * local : (k + 1) * local, :] = basis_ref[k]
    con_ref[...] = mm(hot, rows_ref[...], NT).astype(bf16)
    for p in range(groups):
        base = pl.multiple_of((m ^ p) * quarter, quarter)
        for k in range(comps):
            outs[p][k * local : (k + 1) * local, :] = basis_ref[k, :, pl.ds(base, quarter)]


def elastic_kernel(groups, *refs):
    msgs = refs[:groups]
    stiff_ref = refs[groups]
    own_ref, qs_ref = refs[groups + 1], refs[groups + 2]
    outs = refs[groups + 3 : groups + 2 + groups]
    right_ref, left_ref = refs[groups + 2 + groups :]
    quarter = msgs[0].shape[1]
    local = own_ref.shape[0] - 8
    comps = 3
    m = lax.axis_index("modes")
    disp = []
    for k in range(comps):
        total = None
        for p in range(groups):
            q_rows = msgs[p][comps * local : comps * local + 16, :local]
            term = mm(q_rows, msgs[p][k * local : (k + 1) * local, :], NN)
            total = term if total is None else total + term
        disp.append(total[0:1] + total[1:2] + total[2:3])
    for p in range(groups):
        qs_ref[:, p * local : (p + 1) * local] = msgs[p][comps * local : comps * local + 16, :local]
    square = 1.0 + (disp[0] * disp[0] + disp[1] * disp[1] + disp[2] * disp[2])
    radius = jnp.sqrt(square)
    base = pl.multiple_of(m * quarter, quarter)
    spring_rate = stiff_ref[:, pl.ds(base, quarter)] / radius
    curvature_rate = -spring_rate / (radius * radius)
    for p in range(groups):
        rows = slice(p * local, (p + 1) * local)
        projected = None
        for k in range(comps):
            block = msgs[p][k * local : (k + 1) * local, :]
            wide = block.astype(f32)
            right_ref[rows, k * quarter : (k + 1) * quarter] = block
            left_ref[rows, k * quarter : (k + 1) * quarter] = (spring_rate * wide).astype(bf16)
            term = wide * disp[k]
            projected = term if projected is None else projected + term
        right_ref[rows, comps * quarter :] = projected.astype(bf16)
        left_ref[rows, comps * quarter :] = (curvature_rate * projected).astype(bf16)
    hess = mm(left_ref[...], right_ref[...], NT)
    force = [spring_rate * d for d in disp]
    force_rows = jnp.concatenate([stack_rows(parts_of(f), 16) for f in force], axis=1)
    grads = mm(force_rows, right_ref[:, : comps * quarter], NT)
    grad = grads[0:1] + grads[1:2] + grads[2:3]
    width = groups * local
    own_ref[:local, :] = hess[:local]
    own_ref[local:, :] = stack_rows([permute_static(grad, 0, groups, local)], 8)
    for p in range(1, groups):
        out = outs[p - 1]
        out[:local, :] = permute_static(
            hess[p * local : (p + 1) * local], p, groups, local
        ).astype(bf16)
        out[local:, :] = stack_rows(
            parts_of(permute_static(grad, p, groups, local)), 16
        )


def contact_kernel(groups, slot_count, *refs):
    blocks = refs[:groups]
    con_ref = refs[0]
    qs_ref, peer_ref, slot_ref, count_ref = refs[groups : groups + 4]
    out_ref, right_ref, left_ref = refs[groups + 4 :]
    nodes = con_ref.shape[0]
    local = out_ref.shape[0] - 8
    comps = 3
    pairs = peer_ref.shape[1]
    position = lax.broadcasted_iota(jnp.int32, (1, pairs), 1)
    live = position < count_ref[0]
    ends = peer_ref[...] * slot_count + slot_ref[...]
    node = lax.broadcasted_iota(jnp.int32, (nodes, pairs), 0)
    first = jnp.where((node == ends[0:1]) & live, 1.0, 0.0)
    second = jnp.where((node == ends[1:2]) & live, 1.0, 0.0)
    edge = (first - second).astype(bf16)
    lane = lax.broadcasted_iota(jnp.int32, (16, local), 1)
    row = lax.broadcasted_iota(jnp.int32, (16, local), 0)
    pick = jnp.where((lane >= 3 * row) & (lane < 3 * row + 3), 1.0, 0.0).astype(bf16)
    rest = mm(pick, con_ref[:, comps * local :], NT)
    rows = []
    for k in range(comps):
        total = None
        for p in range(groups):
            term = mm(
                qs_ref[:, p * local : (p + 1) * local],
                blocks[p][:nodes, k * local : (k + 1) * local],
                NT,
            )
            total = term if total is None else total + term
        moved = total[0:1] + total[1:2] + total[2:3]
        rows += parts_of(rest[k : k + 1] + moved)
    gaps = mm(stack_rows(rows, 16), edge, NN)
    sep = [gaps[3 * k : 3 * k + 1] + gaps[3 * k + 1 : 3 * k + 2] + gaps[3 * k + 2 : 3 * k + 3] for k in range(comps)]
    distance = sep[0] * sep[0] + sep[1] * sep[1] + sep[2] * sep[2] + gap_offset
    slope, bend = barrier_slopes(distance)
    active = jnp.where(live, 1.0, 0.0)
    slope = slope * active
    bend = bend * active
    for p in range(groups):
        diff = mm(blocks[p][:nodes, : comps * local], edge, TN)
        rows_p = slice(p * local, (p + 1) * local)
        leverage = None
        for k in range(comps):
            part = diff[k * local : (k + 1) * local]
            right_ref[rows_p, k * pairs : (k + 1) * pairs] = part.astype(bf16)
            if p == 0:
                left_ref[:, k * pairs : (k + 1) * pairs] = (2.0 * slope * part).astype(bf16)
            term = part * sep[k]
            leverage = term if leverage is None else leverage + term
        right_ref[rows_p, comps * pairs :] = leverage.astype(bf16)
        if p == 0:
            left_ref[:, comps * pairs :] = (4.0 * bend * leverage).astype(bf16)
    out_ref[:local, :] = mm(left_ref[...], right_ref[...], NT)
    force_rows = []
    for k in range(comps):
        force_rows += parts_of(2.0 * slope * sep[k])
    spread = mm(stack_rows(force_rows, 16), edge, NT)
    node_rows = []
    for k in range(comps):
        node_rows += parts_of(spread[3 * k : 3 * k + 1] + spread[3 * k + 1 : 3 * k + 2] + spread[3 * k + 2 : 3 * k + 3])
    pulled = mm(stack_rows(node_rows, 16), con_ref[:, : comps * local], NN)
    grad = jnp.zeros((1, local), f32)
    for k in range(comps):
        for i in range(3):
            grad = grad + pulled[3 * k + i : 3 * k + i + 1, k * local : (k + 1) * local]
    grad = jnp.concatenate([grad, jnp.zeros((1, out_ref.shape[1] - local), f32)], axis=1)
    out_ref[local:, :] = stack_rows([grad], 8)


def pack(hess, grad, out_ref):
    local = hess.shape[0]
    out_ref[:local, :] = hess.astype(bf16)
    out_ref[local:, :] = stack_rows(parts_of(grad), 16)


def merge_kernel(groups, factor, own_ref, contact_ref, *refs):
    gots, out_ref = refs[: groups - 1], refs[groups - 1]
    local = own_ref.shape[0] - 8
    m = lax.axis_index("modes")
    hess = own_ref[:local, :] + contact_ref[:local, :]
    grad = own_ref[local : local + 1, :] + contact_ref[local : local + 1, :]
    for got in gots:
        hess = hess + got[:local, :].astype(f32)
        rows = got[local:, :].astype(f32)
        grad = grad + (rows[0:1] + (rows[1:2] + rows[2:3]))
    hess = permute_traced(hess, m, groups, local)
    pack(hess * factor, grad * factor, out_ref)


def sum_kernel(one_ref, two_ref, *refs):
    local = one_ref.shape[0] - 16
    hess = one_ref[:local, :].astype(f32) + two_ref[:local, :].astype(f32)
    rows = one_ref[local:, :].astype(f32) + two_ref[local:, :].astype(f32)
    grad = rows[0:1] + (rows[1:2] + rows[2:3])
    if len(refs) == 1:
        pack(hess, grad, refs[0])
        return
    hess_hbm, grad_hbm, hess_ref, grad_ref, sems = refs
    grad_ref[...] = grad[:, : grad_ref.shape[1]]
    second = pltpu.make_async_copy(grad_ref, grad_hbm, sems.at[1])
    second.start()
    hess_ref[...] = hess
    first = pltpu.make_async_copy(hess_ref, hess_hbm, sems.at[0])
    first.start()
    second.wait()
    first.wait()


def body(
    reduced_coords, mode_basis, rest_shape, stiffness, send_slots, pair_peer, pair_slot, pair_count
):
    local, comps, count = mode_basis.shape
    peers = lax.axis_size("verts")
    groups = lax.axis_size("modes")
    modes = local * groups
    factor = modes / (3.0 * count * peers)
    quarter = count // groups
    slot_count = send_slots.shape[2]
    nodes = peers * slot_count
    pairs = pair_peer.shape[2]
    msg_rows = comps * local + 16
    wide = (comps + 1) * local

    def swap(x, axis, step):
        size = lax.axis_size(axis)
        return lax.ppermute(x, axis, [(i, i ^ step) for i in range(size)])

    def limit(n):
        return pltpu.CompilerParams(vmem_limit_bytes=n)

    big = nodes > 256
    *mine, contact = pl.pallas_call(
        lambda *refs: select_kernel(groups, *refs),
        out_shape=[jax.ShapeDtypeStruct((msg_rows, quarter), bf16)] * groups
        + [jax.ShapeDtypeStruct((nodes, wide), bf16)],
        in_specs=[HB] * 4,
        out_specs=[VM] * (groups + 1),
        scratch_shapes=[
            pltpu.VMEM((wide, count), bf16),
            pltpu.VMEM((1, local), f32),
            pltpu.VMEM((comps, local, count), bf16),
            pltpu.VMEM((comps, count), f32),
            pltpu.VMEM((peers, slot_count), jnp.int32),
            pltpu.SemaphoreType.DMA((4,)),
        ],
        compiler_params=limit((40 if big else 8) << 20),
        name="select",
    )(
        *[
            pltpu.with_memory_space_constraint(x, pltpu.HBM)
            for x in (
                reduced_coords.reshape(1, local),
                jnp.transpose(mode_basis, (1, 0, 2)),
                rest_shape,
                send_slots[0],
            )
        ]
    )
    contact = lax.all_to_all(
        contact.reshape(peers, slot_count, wide), "verts", split_axis=0, concat_axis=0, tiled=True
    ).reshape(nodes, wide)
    basis = [mine[0]] + [swap(mine[p], "modes", p) for p in range(1, groups)]
    nodes_of = [contact] + [swap(contact, "modes", p) for p in range(1, groups)]
    own, coords, *sends = pl.pallas_call(
        lambda *refs: elastic_kernel(groups, *refs),
        out_shape=[
            jax.ShapeDtypeStruct((local + 8, modes), f32),
            jax.ShapeDtypeStruct((16, modes), bf16),
        ]
        + [jax.ShapeDtypeStruct((local + 16, modes), bf16)] * (groups - 1),
        in_specs=[VM] * (groups + 1),
        out_specs=[VM] * (groups + 1),
        scratch_shapes=[pltpu.VMEM((modes, (comps + 1) * quarter), bf16)] * 2,
        compiler_params=limit((40 if big else 8) << 20),
        cost_estimate=pl.CostEstimate(flops=10**9, bytes_accessed=10**6, transcendentals=0),
        name="elastic",
    )(*basis, stiffness.reshape(1, count))
    got = [swap(sends[p - 1], "modes", p) for p in range(1, groups)]
    touched = pl.pallas_call(
        lambda *refs: contact_kernel(groups, slot_count, *refs),
        out_shape=jax.ShapeDtypeStruct((local + 8, modes), f32),
        in_specs=[VM] * (groups + 3) + [SM],
        out_specs=VM,
        scratch_shapes=[
            pltpu.VMEM((modes, (comps + 1) * pairs), bf16),
            pltpu.VMEM((local, (comps + 1) * pairs), bf16),
        ],
        compiler_params=limit((56 if big else 16) << 20),
        cost_estimate=pl.CostEstimate(flops=2 * 10**9, bytes_accessed=2 * 10**6, transcendentals=0),
        name="contact",
    )(*nodes_of, coords, pair_peer[0], pair_slot[0], pair_count)
    total = pl.pallas_call(
        lambda *refs: merge_kernel(groups, factor, *refs),
        out_shape=jax.ShapeDtypeStruct((local + 16, modes), bf16),
        in_specs=[VM] * (groups + 1),
        out_specs=VM,
        compiler_params=limit(4 << 20),
        name="merge",
    )(own, touched, *got)
    step = 1
    while 2 * step < peers:
        total = pl.pallas_call(
            sum_kernel,
            out_shape=jax.ShapeDtypeStruct((local + 16, modes), bf16),
            in_specs=[VM] * 2,
            out_specs=VM,
            compiler_params=limit(4 << 20),
            name="add",
        )(total, swap(total, "verts", step))
        step *= 2
    hess, grad = pl.pallas_call(
        sum_kernel,
        out_shape=[jax.ShapeDtypeStruct((local, modes), f32), jax.ShapeDtypeStruct((1, local), f32)],
        in_specs=[VM] * 2,
        out_specs=[HB] * 2,
        scratch_shapes=[
            pltpu.VMEM((local, modes), f32),
            pltpu.VMEM((1, local), f32),
            pltpu.SemaphoreType.DMA((2,)),
        ],
        compiler_params=limit(4 << 20),
        name="last",
    )(total, swap(total, "verts", step))
    return (hess, grad.reshape(local))


def solution(mesh):
    return jax.shard_map(
        body,
        mesh=mesh,
        in_specs=(
            P("modes"),
            P("modes", None, "verts"),
            P(None, "verts"),
            P("verts"),
            P("verts", None, None),
            P("verts", None, None),
            P("verts", None, None),
            P("verts"),
        ),
        out_specs=(P("modes", None), P("modes")),
        check_vma=False,
    )
```

```python
import jax
import jax.numpy as jnp
from jax import lax
from jax.experimental import pallas as pl
from jax.experimental.pallas import tpu as pltpu
from jax.sharding import PartitionSpec as P


barrier_reach = 1.5
gap_offset = 0.1
f32, bf16 = jnp.float32, jnp.bfloat16

NT = (((1,), (1,)), ((), ()))
NN = (((1,), (0,)), ((), ()))
VM = pl.BlockSpec(memory_space=pltpu.VMEM)
SM = pl.BlockSpec(memory_space=pltpu.SMEM)
HB = pl.BlockSpec(memory_space=pltpu.HBM)


def mm(a, b, dims):
    return lax.dot_general(a, b, dims, preferred_element_type=f32)


def parts_of(x):
    high = x.astype(bf16)
    rest = x - high.astype(f32)
    middle = rest.astype(bf16)
    low = (rest - middle.astype(f32)).astype(bf16)
    return [high, middle, low]


def stack_rows(rows, count):
    width = rows[0].shape[1]
    have = len(rows)
    return jnp.concatenate(rows + [jnp.zeros((count - have, width), rows[0].dtype)], axis=0)


def barrier_slopes(distance):
    excess = distance - barrier_reach
    ratio_log = jnp.log(distance / barrier_reach)
    slope_term = -(2.0 * excess * ratio_log + excess * excess / distance)
    curvature = -(
        2.0 * ratio_log + 4.0 * excess / distance - excess * excess / (distance * distance)
    )
    inside = distance < barrier_reach
    return (jnp.where(inside, slope_term, 0.0), jnp.where(inside, curvature, 0.0))


def swap_blocks(h, step, width):
    size = step * width
    pieces = [h[:, i : i + size] for i in range(0, h.shape[1], size)]
    order = [pieces[i ^ 1] for i in range(len(pieces))]
    return jnp.concatenate(order, axis=1)


def permute_static(h, p, groups, width):
    step = 1
    while step < groups:
        if p & step:
            h = swap_blocks(h, step, width)
        step *= 2
    return h


def permute_traced(h, m, groups, width):
    step = 1
    while step < groups:
        h = jnp.where((m & step) != 0, swap_blocks(h, step, width), h)
        step *= 2
    return h


def block_order(peers):
    order, step = [0], peers // 2
    while step >= 1:
        order = [v for v in order] + [v | step for v in order]
        step //= 2
    return order


def make_edges(slot_count, peer_ref, slot_ref, edge_ref):
    nodes, pairs = edge_ref.shape
    ends = (peer_ref[...] ^ lax.axis_index("verts")) * slot_count + slot_ref[...]
    node = lax.broadcasted_iota(jnp.int32, (nodes, pairs), 0)
    edge = jnp.where(node == ends[0:1], 1.0, 0.0) - jnp.where(node == ends[1:2], 1.0, 0.0)
    edge_ref[...] = edge.astype(bf16)


def select_kernel(groups, *refs):
    sources, outs = refs[:7], refs[7 : 7 + groups]
    keep_ref, send_ref, edge_ref, stiff_out, rows_ref = refs[7 + groups : 12 + groups]
    held, sems = refs[12 + groups : -1], refs[-1]
    slots_ref, peer_ref, pair_ref, rest_ref, q_ref, stiff_ref, basis_ref = held
    comps, local, count = basis_ref.shape
    quarter = count // groups
    copies = [
        pltpu.make_async_copy(source, target, sems.at[i])
        for i, (source, target) in enumerate(zip(sources, held))
    ]
    for copy in copies:
        copy.start()
    copies[0].wait()
    peers, slot_count = slots_ref.shape
    a = lax.axis_index("verts")
    slots = jnp.concatenate(
        [slots_ref[pl.ds(a ^ other, 1), :] for other in block_order(peers)], axis=0
    )
    spread = jnp.broadcast_to(slots[:, None, :], (peers, slot_count, slot_count))
    pick = lax.broadcasted_iota(jnp.int32, spread.shape, 1) == lax.broadcasted_iota(
        jnp.int32, spread.shape, 2
    )
    column = jnp.sum(jnp.where(pick, spread, 0).astype(f32), axis=2, keepdims=True)
    column = column.reshape(peers * slot_count, 1).astype(jnp.int32)
    hot = lax.broadcasted_iota(jnp.int32, (peers * slot_count, count), 1) == column
    hot = jnp.where(hot, 1.0, 0.0).astype(bf16)
    for i in (1, 2):
        copies[i].wait()
    make_edges(slot_count, peer_ref, pair_ref, edge_ref)
    copies[3].wait()
    rest_rows = []
    for k in range(comps):
        rest_rows += parts_of(rest_ref[k : k + 1, :])
    rows_ref[comps * local :, :] = stack_rows(rest_rows, rows_ref.shape[0] - comps * local)
    copies[4].wait()
    m = lax.axis_index("modes")
    q_rows = stack_rows(parts_of(q_ref[...]), 8)
    q_rows = jnp.concatenate([q_rows, jnp.zeros((8, quarter - local), bf16)], axis=1)
    for p in range(groups):
        outs[p][comps * local :, :] = q_rows
    copies[5].wait()
    stiff_out[...] = stiff_ref[:, pl.ds(pl.multiple_of(m * quarter, quarter), quarter)]
    copies[6].wait()
    for k in range(comps):
        rows_ref[k * local : (k + 1) * local, :] = basis_ref[k]
    picked = mm(hot, rows_ref[...], NT).astype(bf16)
    half = picked.shape[0] // 2
    keep_ref[...] = picked[:half]
    send_ref[...] = picked[half:]
    for p in range(groups):
        base = pl.multiple_of((m ^ p) * quarter, quarter)
        for k in range(comps):
            outs[p][k * local : (k + 1) * local, :] = basis_ref[k, :, pl.ds(base, quarter)]


def elastic_kernel(groups, *refs):
    msgs = refs[:groups]
    stiff_ref = refs[groups]
    own_ref, qs_ref = refs[groups + 1], refs[groups + 2]
    outs = refs[groups + 3 : groups + 2 + groups]
    right_ref, left_ref = refs[groups + 2 + groups :]
    quarter = msgs[0].shape[1]
    local = own_ref.shape[0] - 8
    comps = 3
    disp = []
    for k in range(comps):
        total = None
        for p in range(groups):
            q_rows = msgs[p][comps * local :, :local]
            term = mm(q_rows, msgs[p][k * local : (k + 1) * local, :], NN)
            total = term if total is None else total + term
        disp.append(total[0:1] + total[1:2] + total[2:3])
    for p in range(groups):
        qs_ref[:, p * local : (p + 1) * local] = msgs[p][comps * local :, :local]
    square = 1.0 + (disp[0] * disp[0] + disp[1] * disp[1] + disp[2] * disp[2])
    radius = jnp.sqrt(square)
    spring_rate = stiff_ref[...] / radius
    curvature_rate = -spring_rate / (radius * radius)
    for p in range(groups):
        rows = slice(p * local, (p + 1) * local)
        projected = None
        for k in range(comps):
            block = msgs[p][k * local : (k + 1) * local, :]
            wide = block.astype(f32)
            right_ref[rows, k * quarter : (k + 1) * quarter] = block
            left_ref[rows, k * quarter : (k + 1) * quarter] = (spring_rate * wide).astype(bf16)
            term = wide * disp[k]
            projected = term if projected is None else projected + term
        right_ref[rows, comps * quarter :] = projected.astype(bf16)
        left_ref[rows, comps * quarter :] = (curvature_rate * projected).astype(bf16)
    hess = mm(left_ref[...], right_ref[...], NT)
    force = [spring_rate * d for d in disp]
    force_rows = jnp.concatenate([stack_rows(parts_of(f), 16) for f in force], axis=1)
    grads = mm(force_rows, right_ref[:, : comps * quarter], NT)
    grad = grads[0:1] + grads[1:2] + grads[2:3]
    own_ref[:local, :] = hess[:local]
    own_ref[local:, :] = stack_rows([permute_static(grad, 0, groups, local)], 8)
    for p in range(1, groups):
        out = outs[p - 1]
        out[:local, :] = permute_static(
            hess[p * local : (p + 1) * local], p, groups, local
        ).astype(bf16)
        out[local:, :] = stack_rows(
            parts_of(permute_static(grad, p, groups, local)), 8
        )


def turn_kernel(kept_ref, got_ref, rows_ref, rest_ref):
    both = jnp.concatenate([kept_ref[...], got_ref[...]], axis=0).astype(f32)
    turned = jnp.transpose(both)
    count = rows_ref.shape[0]
    rows_ref[...] = turned[:count].astype(bf16)
    rest = turned[count : count + 16]
    rest_rows = [rest[3 * k : 3 * k + 1] + (rest[3 * k + 1 : 3 * k + 2] + rest[3 * k + 2 : 3 * k + 3]) for k in range(3)]
    rest_ref[...] = stack_rows(rest_rows, 8)


def contact_kernel(groups, slot_count, *refs):
    arrived = refs[:groups]
    nodes = arrived[0].shape[1]
    origin = lax.div(lax.broadcasted_iota(jnp.int32, (1, nodes), 1), slot_count)
    odd, bit = origin, 1
    while bit * slot_count < nodes:
        odd = odd ^ (origin >> bit)
        bit += 1
    crossed = (odd & 1).astype(f32)
    direct = (1.0 - crossed).astype(bf16)
    crossed = crossed.astype(bf16)
    blocks = [arrived[p][...] * direct + arrived[p ^ 1][...] * crossed for p in range(groups)]
    rest_ref, qs_ref, edge_ref, count_ref = refs[groups : groups + 4]
    out_ref, right_ref, left_ref = refs[groups + 4 :]
    local = out_ref.shape[0] - 8
    comps = 3
    pairs = edge_ref.shape[1]
    edge = edge_ref[...]
    rows = []
    for k in range(comps):
        total = None
        for p in range(groups):
            term = mm(
                qs_ref[:, p * local : (p + 1) * local],
                blocks[p][k * local : (k + 1) * local],
                NN,
            )
            total = term if total is None else total + term
        moved = total[0:1] + total[1:2] + total[2:3]
        rows += parts_of(rest_ref[k : k + 1, :] + moved)
    gaps = mm(stack_rows(rows, 16), edge, NN)
    sep = [gaps[3 * k : 3 * k + 1] + gaps[3 * k + 1 : 3 * k + 2] + gaps[3 * k + 2 : 3 * k + 3] for k in range(comps)]
    distance = sep[0] * sep[0] + sep[1] * sep[1] + sep[2] * sep[2] + gap_offset
    slope, bend = barrier_slopes(distance)
    live = lax.broadcasted_iota(jnp.int32, (1, pairs), 1) < count_ref[...]
    active = jnp.where(live, 1.0, 0.0)
    slope = slope * active
    bend = bend * active
    for p in range(groups):
        diff = mm(blocks[p], edge, NN)
        rows_p = slice(p * local, (p + 1) * local)
        leverage = None
        for k in range(comps):
            part = diff[k * local : (k + 1) * local]
            right_ref[rows_p, k * pairs : (k + 1) * pairs] = part.astype(bf16)
            if p == 0:
                left_ref[:, k * pairs : (k + 1) * pairs] = (2.0 * slope * part).astype(bf16)
            term = part * sep[k]
            leverage = term if leverage is None else leverage + term
        right_ref[rows_p, comps * pairs :] = leverage.astype(bf16)
        if p == 0:
            left_ref[:, comps * pairs :] = (4.0 * bend * leverage).astype(bf16)
    out_ref[:local, :] = mm(left_ref[...], right_ref[...], NT)
    force_rows = []
    for k in range(comps):
        force_rows += parts_of(2.0 * slope * sep[k])
    spread = mm(stack_rows(force_rows, 16), edge, NT)
    node_rows = []
    for k in range(comps):
        node_rows += parts_of(spread[3 * k : 3 * k + 1] + spread[3 * k + 1 : 3 * k + 2] + spread[3 * k + 2 : 3 * k + 3])
    pulled = mm(stack_rows(node_rows, 16), blocks[0], NT)
    grad = jnp.zeros((1, local), f32)
    for k in range(comps):
        for i in range(3):
            grad = grad + pulled[3 * k + i : 3 * k + i + 1, k * local : (k + 1) * local]
    grad = jnp.concatenate([grad, jnp.zeros((1, out_ref.shape[1] - local), f32)], axis=1)
    out_ref[local:, :] = stack_rows([grad], 8)


def pack(hess, grad, out_ref):
    local = hess.shape[0]
    out_ref[:local, :] = hess.astype(bf16)
    out_ref[local:, :] = stack_rows(parts_of(grad), 8)


def merge_kernel(groups, factor, own_ref, contact_ref, *refs):
    gots, out_ref = refs[: groups - 1], refs[groups - 1]
    local = own_ref.shape[0] - 8
    m = lax.axis_index("modes")
    hess = own_ref[:local, :] + contact_ref[:local, :]
    grad = own_ref[local : local + 1, :] + contact_ref[local : local + 1, :]
    for got in gots:
        hess = hess + got[:local, :].astype(f32)
        rows = got[local:, :].astype(f32)
        grad = grad + (rows[0:1] + (rows[1:2] + rows[2:3]))
    hess = permute_traced(hess, m, groups, local)
    pack(hess * factor, grad * factor, out_ref)


def sum_kernel(one_ref, two_ref, *refs):
    local = one_ref.shape[0] - 8
    hess = one_ref[:local, :].astype(f32) + two_ref[:local, :].astype(f32)
    rows = one_ref[local:, :].astype(f32) + two_ref[local:, :].astype(f32)
    grad = rows[0:1] + (rows[1:2] + rows[2:3])
    if len(refs) == 1:
        pack(hess, grad, refs[0])
        return
    hess_hbm, grad_hbm, hess_ref, grad_ref, sems = refs
    grad_ref[...] = grad[:, : grad_ref.shape[1]]
    second = pltpu.make_async_copy(grad_ref, grad_hbm, sems.at[1])
    second.start()
    hess_ref[...] = hess
    first = pltpu.make_async_copy(hess_ref, hess_hbm, sems.at[0])
    first.start()
    second.wait()
    first.wait()


def body(
    reduced_coords, mode_basis, rest_shape, stiffness, send_slots, pair_peer, pair_slot, pair_count
):
    local, comps, count = mode_basis.shape
    peers = lax.axis_size("verts")
    groups = lax.axis_size("modes")
    modes = local * groups
    factor = modes / (3.0 * count * peers)
    quarter = count // groups
    slot_count = send_slots.shape[2]
    nodes = peers * slot_count
    pairs = pair_peer.shape[2]
    msg_rows = comps * local + 8
    wide = (comps + 1) * local

    def swap(x, axis, step):
        size = lax.axis_size(axis)
        return lax.ppermute(x, axis, [(i, i ^ step) for i in range(size)])

    def cross(x, step):
        pairs_of = [
            (v * groups + m, (v ^ step) * groups + (m ^ 1))
            for v in range(peers)
            for m in range(groups)
        ]
        return lax.ppermute(x, ("verts", "modes"), pairs_of)

    def limit(n):
        return pltpu.CompilerParams(vmem_limit_bytes=n)

    big = nodes > 256
    sources = (
        send_slots[0],
        pair_peer[0],
        pair_slot[0],
        rest_shape,
        reduced_coords.reshape(1, local),
        stiffness.reshape(1, count),
        jnp.transpose(mode_basis, (1, 0, 2)),
    )
    *mine, keep, send, edge, stiff = pl.pallas_call(
        lambda *refs: select_kernel(groups, *refs),
        out_shape=[jax.ShapeDtypeStruct((msg_rows, quarter), bf16)] * groups
        + [jax.ShapeDtypeStruct((nodes // 2, wide), bf16)] * 2
        + [
            jax.ShapeDtypeStruct((nodes, pairs), bf16),
            jax.ShapeDtypeStruct((1, quarter), f32),
        ],
        in_specs=[HB] * 7,
        out_specs=[VM] * (groups + 4),
        scratch_shapes=[pltpu.VMEM((wide, count), bf16)]
        + [
            pltpu.VMEM(x.shape, x.dtype)
            for x in sources
        ]
        + [pltpu.SemaphoreType.DMA((7,))],
        compiler_params=limit((56 if big else 8) << 20),
        name="select",
    )(*[pltpu.with_memory_space_constraint(x, pltpu.HBM) for x in sources])
    kept, send = [keep], [send]
    step, blocks = 1, peers // 2
    while True:
        got = cross(jnp.concatenate(send, axis=0), step)
        if blocks == 1:
            break
        size = blocks * slot_count
        pieces = kept + [got[i : i + size] for i in range(0, got.shape[0], size)]
        kept = [piece[: size // 2] for piece in pieces]
        send = [piece[size // 2 :] for piece in pieces]
        step, blocks = 2 * step, blocks // 2
    contact, rest = pl.pallas_call(
        turn_kernel,
        out_shape=[
            jax.ShapeDtypeStruct((comps * local, nodes), bf16),
            jax.ShapeDtypeStruct((8, nodes), f32),
        ],
        in_specs=[VM] * 2,
        out_specs=[VM] * 2,
        compiler_params=limit((16 if big else 4) << 20),
        name="turn",
    )(jnp.concatenate(kept, axis=0), got)
    basis = [mine[0]] + [swap(mine[p], "modes", p) for p in range(1, groups)]
    nodes_of = [contact] + [swap(contact, "modes", p) for p in range(1, groups)]
    elastic = pl.pallas_call(
        lambda *refs: elastic_kernel(groups, *refs),
        out_shape=[
            jax.ShapeDtypeStruct((local + 8, modes), f32),
            jax.ShapeDtypeStruct((8, modes), bf16),
        ]
        + [jax.ShapeDtypeStruct((local + 8, modes), bf16)] * (groups - 1),
        in_specs=[VM] * (groups + 1),
        out_specs=[VM] * (groups + 1),
        scratch_shapes=[pltpu.VMEM((modes, (comps + 1) * quarter), bf16)] * 2,
        compiler_params=limit((40 if big else 8) << 20),
        cost_estimate=pl.CostEstimate(flops=10**9, bytes_accessed=10**6, transcendentals=0),
        name="elastic",
    )
    own, coords, *sends = elastic(*basis, stiff)
    got = [swap(sends[p - 1], "modes", p) for p in range(1, groups)]
    touched = pl.pallas_call(
        lambda *refs: contact_kernel(groups, slot_count, *refs),
        out_shape=jax.ShapeDtypeStruct((local + 8, modes), f32),
        in_specs=[VM] * (groups + 4),
        out_specs=VM,
        scratch_shapes=[
            pltpu.VMEM((modes, (comps + 1) * pairs), bf16),
            pltpu.VMEM((local, (comps + 1) * pairs), bf16),
        ],
        compiler_params=limit((56 if big else 16) << 20),
        cost_estimate=pl.CostEstimate(flops=2 * 10**9, bytes_accessed=2 * 10**6, transcendentals=0),
        name="contact",
    )(*nodes_of, rest, coords, edge, pair_count.reshape(1, 1))
    total = pl.pallas_call(
        lambda *refs: merge_kernel(groups, factor, *refs),
        out_shape=jax.ShapeDtypeStruct((local + 8, modes), bf16),
        in_specs=[VM] * (groups + 1),
        out_specs=VM,
        compiler_params=limit(4 << 20),
        name="merge",
    )(own, touched, *got)
    step = 1
    while 2 * step < peers:
        total = pl.pallas_call(
            sum_kernel,
            out_shape=jax.ShapeDtypeStruct((local + 8, modes), bf16),
            in_specs=[VM] * 2,
            out_specs=VM,
            compiler_params=limit(4 << 20),
            name="add",
        )(total, swap(total, "verts", step))
        step *= 2
    hess, grad = pl.pallas_call(
        sum_kernel,
        out_shape=[jax.ShapeDtypeStruct((local, modes), f32), jax.ShapeDtypeStruct((1, local), f32)],
        in_specs=[VM] * 2,
        out_specs=[HB] * 2,
        scratch_shapes=[
            pltpu.VMEM((local, modes), f32),
            pltpu.VMEM((1, local), f32),
            pltpu.SemaphoreType.DMA((2,)),
        ],
        compiler_params=limit(4 << 20),
        name="last",
    )(total, swap(total, "verts", step))
    return (hess, grad.reshape(local))


def solution(mesh):
    return jax.shard_map(
        body,
        mesh=mesh,
        in_specs=(
            P("modes"),
            P("modes", None, "verts"),
            P(None, "verts"),
            P("verts"),
            P("verts", None, None),
            P("verts", None, None),
            P("verts", None, None),
            P("verts"),
        ),
        out_specs=(P("modes", None), P("modes")),
        check_vma=False,
    )
```
